128 devices in a mesh: leaf: 16 (over x, z), panel: 8 (over y, core).
Axes of the slice: x: 4, y: 4, z: 4, core: 2. Of those that a mesh axis runs over, the one named last changes fastest.
Arguments:
- adjoint_rhs: float32 [16, 64, 3968], P('leaf', None, 'panel'), may hold values from -6 to 6
- panel_tiles: bfloat16 [16, 2048, 12544], P('leaf', 'panel'), may hold values from -0.0625 to 0.0625
- diag_inverse: bfloat16 [16, 3968, 2048], P('leaf', 'panel'), may hold values from -0.125 to 0.125
- front_sizes: int32 [31], replicated, may hold values from 512 to 2048
Outputs:
- solution: float32 [16, 5, 64, 2048], P('leaf', None, None, 'panel')
The draws below stay inside these ranges and needn't reach their ends.
All inputs are finite; a program needn't handle non-finite values.
Results may differ from the reference program's by a relative error of at most 0.0051.
Values sent between devices are 32-bit elements; how exact they have to be, the bound alone decides.
A program may use at most 128 MiB of HBM per device.

```python
import jax
import jax.numpy as jnp
from jax import lax

SEP = 2048
NRHS = 64
LEVELS = 5
NODES = 31
PCOLS = 12544
DROWS = 3968
N_LEAF = 16
N_PANEL = 8


def plant(drawn, own_key, low, top_value):
    index_at = [jax.random.randint(jax.random.fold_in(own_key, axis), (), 0, length) for axis, length in enumerate(drawn.shape)]
    main_axis = drawn.shape.index(max(drawn.shape))
    neighbour = index_at[:main_axis] + [(index_at[main_axis] + 1) % drawn.shape[main_axis]] + index_at[main_axis + 1:]
    return drawn.at[tuple(index_at)].set(low).at[tuple(neighbour)].set(top_value)


def shard_levels(stream_key, shape, pieces, smallest, high):
    def one(axis_at, shards_of):
        heights = jax.random.uniform(jax.random.fold_in(jax.random.fold_in(stream_key, 6), axis_at), (shards_of,), jnp.float32, smallest / len(pieces), high / len(pieces))
        return jnp.repeat(jnp.exp(heights), shape[axis_at] // shards_of).reshape((-1,) + (1,) * (len(shape) - axis_at - 1))

    factor_of = one(*pieces[0])
    for cut in pieces[1:]:
        factor_of = factor_of * one(*cut)
    return factor_of


def centred(own_key, shape, deviation, limit, pieces=(), kind=jnp.bfloat16):
    drawn = deviation * jax.random.normal(own_key, shape, jnp.float32)
    if pieces:
        drawn = drawn * shard_levels(own_key, shape, pieces, -0.22, 0.18)
    return jnp.clip(drawn, -limit, limit).astype(kind)


def setup_inputs(seed: int = 0) -> dict:
    key_of = jax.random.split(jax.random.key(seed), 5)
    adjoint_rhs = centred(key_of[0], (N_LEAF, NRHS, DROWS), 1.0, 6.0, ((0, 16), (2, 8)), jnp.float32)
    panel_tiles = centred(key_of[1], (N_LEAF, SEP, PCOLS), (4 * SEP) ** -0.5, 0.0625, ((0, 16), (1, 8)))
    diag_inverse = centred(key_of[2], (N_LEAF, DROWS, SEP), SEP ** -0.5, 0.125, ((0, 16), (1, 8)))
    front_sizes = plant(jax.random.randint(key_of[3], (NODES,), SEP // 4, SEP + 1), jax.random.fold_in(key_of[3], 1), SEP // 4, SEP).astype(jnp.int32)
    return {"adjoint_rhs": adjoint_rhs, "panel_tiles": panel_tiles, "diag_inverse": diag_inverse, "front_sizes": front_sizes}


def ancestor_terms(pair):
    anc_blocks, tile_blocks = pair
    total = jnp.zeros((anc_blocks.shape[1], tile_blocks.shape[2]), jnp.float32)
    for upper in range(anc_blocks.shape[0]):
        total = total + jnp.dot(anc_blocks[upper], tile_blocks[upper], preferred_element_type=jnp.float32)
    return total


def apply_inverse(pair):
    return jnp.dot(pair[0], pair[1], preferred_element_type=jnp.float32)


def reference(adjoint_rhs, panel_tiles, diag_inverse, front_sizes):
    rows_per = DROWS // N_PANEL
    solved_low = []
    solved_full = []
    positions = jnp.arange(SEP)
    lower_mask = positions[None, :] <= positions[:, None]
    ident = (positions[None, :] == positions[:, None]).astype(jnp.float32)
    for height in range(LEVELS):
        group_size = N_LEAF >> height
        fronts = 1 << height
        col_width = SEP // group_size
        share = col_width // N_PANEL
        col_start = sum(upper * (SEP // (N_LEAF >> upper)) for upper in range(height))
        row_start = sum((SEP // (N_LEAF >> upper)) // N_PANEL for upper in range(height))
        right = adjoint_rhs.reshape(N_LEAF, NRHS, N_PANEL, rows_per)[:, :, :, row_start:row_start + share]
        right = right.reshape(fronts, group_size, NRHS, N_PANEL, share).transpose(0, 2, 1, 3, 4).reshape(fronts, NRHS, SEP)
        right = right.astype(jnp.float32)
        inverse_raw = diag_inverse.reshape(N_LEAF, N_PANEL, rows_per, SEP)[:, :, row_start:row_start + share, :]
        inverse_raw = inverse_raw.reshape(fronts, SEP, SEP).astype(jnp.float32)
        factor = (jnp.where(lower_mask[None], inverse_raw, 0.0) + ident[None]).astype(jnp.bfloat16)
        if height > 0:
            region = panel_tiles[:, :, col_start:col_start + height * col_width]
            region = region.reshape(fronts, group_size, SEP, height, col_width).transpose(0, 3, 2, 1, 4)
            region = region.reshape(fronts, height, SEP, SEP)
            ancestors = jnp.stack([jnp.repeat(solved_low[upper], 1 << (height - upper), axis=0) for upper in range(height)], axis=1)
            resid = right - lax.map(ancestor_terms, (ancestors, region))
        else:
            resid = right
        live_rows = front_sizes[fronts - 1:2 * fronts - 1]
        live = positions[None, None, :] < live_rows[:, None, None]
        resid_low = jnp.where(live, resid, 0.0).astype(jnp.bfloat16)
        solved = lax.map(apply_inverse, (resid_low, factor))
        solved_full.append(solved)
        solved_low.append(solved.astype(jnp.bfloat16))
    return jnp.stack([jnp.repeat(solved_full[height], N_LEAF >> height, axis=0) for height in range(LEVELS)], axis=1)
```

```python
import jax
import jax.numpy as jnp
from jax import lax
from jax.experimental import pallas as pl
from jax.experimental.pallas import tpu as pltpu
from jax.sharding import PartitionSpec as P

MESH = pl.DeviceIdType.MESH
F32, BF16 = jnp.float32, jnp.bfloat16
NP = 8
NL = 16
SEP = 2048
N = 64
STRIP = SEP // NP
LEVELS = 5
G = [NL >> lev for lev in range(LEVELS)]
W = [SEP // g for g in G]
V = [w // NP for w in W]
C = [sum(m * W[m] for m in range(lev)) for lev in range(LEVELS)]
R = [sum(V[m] for m in range(lev)) for lev in range(LEVELS)]
TILES = N // 8 * (STRIP // 128)
GATHER = (0, 1, 2)
SPREAD = (3, 4)
TWO_STEP = (0, 1, 2)


def kernel(*refs):
    refs = list(refs)
    sizes, rhs_hbm, tiles_hbm, diag_hbm, out = refs[:5]
    names = [name for name, _ in scratch()]
    s = dict(zip(names, refs[5:], strict=True))
    me_leaf, me = lax.axis_index("leaf"), lax.axis_index("panel")

    def panel_peer(k):
        return {"panel": lax.rem(me + k, NP)}, lax.rem(me + k, NP)

    def member(lev):
        return lax.rem(me_leaf, G[lev])

    def leaf_peer(lev, k):
        d = member(lev)
        to = lax.rem(d + k, G[lev])
        return {"leaf": me_leaf - d + to}, to

    loads = {}
    done = set()

    def loaded(name):
        if name not in done:
            done.add(name)
            loads[name].wait()

    def load(name, src, dst):
        loads[name] = pltpu.make_async_copy(src, dst, s["load_sem"].at[len(loads)])
        loads[name].start()

    load("rhs", rhs_hbm.at[0], s["rhs"])
    for lev in range(LEVELS):
        rows = pl.ds(R[lev], V[lev])
        load(("diag", lev), diag_hbm.at[0, rows, :], s["diag"].at[rows, :])
        if lev:
            cols = pl.ds(C[lev], lev * W[lev])
            load(("tiles", lev), tiles_hbm.at[0, :, cols], s["tiles"].at[:, cols])

    barrier = pltpu.get_barrier_semaphore()
    for k in range(1, NP):
        pl.semaphore_signal(barrier, inc=1, device_id=panel_peer(k)[0], device_id_type=MESH)
    for k in range(1, NL):
        pl.semaphore_signal(barrier, inc=1, device_id=leaf_peer(0, k)[0], device_id_type=MESH)

    sent = []

    def send(tag, k, src, dst, device):
        copy = pltpu.make_async_remote_copy(
            src_ref=src,
            dst_ref=dst,
            send_sem=s[tag + "_ssem"].at[k - 1],
            recv_sem=s[tag + "_rsem"].at[k - 1],
            device_id=device,
            device_id_type=MESH,
        )
        copy.start()
        sent.append(copy)
        return copy

    def arrive(copies):
        for copy in copies:
            copy.wait_recv()

    def factor_rows(lev):
        loaded(("diag", lev))
        block = s["diag"][R[lev] : R[lev] + V[lev], :].astype(F32)
        row = lax.broadcasted_iota(jnp.int32, (V[lev], SEP), 0)
        row = row + (member(lev) * W[lev] + me * V[lev])
        col = lax.broadcasted_iota(jnp.int32, (V[lev], SEP), 1)
        return jnp.where(col <= row, block, 0.0) + jnp.where(col == row, 1.0, 0.0)

    def send_factor(lev):
        full = factor_rows(lev)
        for q in range(NP):
            s[f"msend{lev}"][q] = full[:, q * STRIP : (q + 1) * STRIP]
        copies = []
        for k in range(1, NP):
            device, to = panel_peer(k)
            copies.append(
                send(f"m{lev}", k, s[f"msend{lev}"].at[to], s[f"mfull{lev}"].at[me], device)
            )
        s[f"mfull{lev}"][me] = s[f"msend{lev}"][me]
        return copies

    def live(lev):
        return sizes[(1 << lev) - 1 + lax.div(me_leaf, G[lev])]

    def put_tiles(ref, value):
        for row in range(N // 8):
            for half in range(STRIP // 128):
                ref[row * 2 + half] = value[row * 8 : row * 8 + 8, half * 128 : half * 128 + 128]

    def get_tiles(ref):
        rows = [
            jnp.concatenate([ref[row * 2], ref[row * 2 + 1]], axis=1) for row in range(N // 8)
        ]
        return jnp.concatenate(rows, axis=0)

    def leaf_sum(lev, value, beside, beside2):
        g, d = G[lev], member(lev)
        if g == 1:
            return value
        if lev not in TWO_STEP:
            s[f"xs{lev}"][...] = value
            copies = []
            for k in range(1, g):
                device, _ = leaf_peer(lev, k)
                copies.append(send(f"xs{lev}", k, s[f"xs{lev}"], s[f"xr{lev}"].at[k - 1], device))
            beside()
            beside2()
            arrive(copies)
            total = value
            for k in range(1, g):
                total = total + s[f"xr{lev}"][k - 1]
            return total
        t = TILES // g
        put_tiles(s[f"xs{lev}"], value)
        copies = []
        for k in range(1, g):
            device, to = leaf_peer(lev, k)
            copies.append(
                send(
                    f"xs{lev}",
                    k,
                    s[f"xs{lev}"].at[pl.ds(to * t, t)],
                    s[f"xr{lev}"].at[k - 1],
                    device,
                )
            )
        beside()
        arrive(copies)
        total = s[f"xs{lev}"][pl.ds(d * t, t)]
        for k in range(1, g):
            total = total + s[f"xr{lev}"][k - 1]
        s[f"xf{lev}"][pl.ds(d * t, t)] = total
        copies = []
        for k in range(1, g):
            device, _ = leaf_peer(lev, k)
            here = s[f"xf{lev}"].at[pl.ds(d * t, t)]
            copies.append(send(f"xf{lev}", k, here, here, device))
        beside2()
        arrive(copies)
        return get_tiles(s[f"xf{lev}"])

    def tile_of(lev, upper):
        start = C[lev] + upper * W[lev]
        return s["tiles"][:, start : start + W[lev]]

    def term(lev, upper, x):
        return jnp.dot(x, tile_of(lev, upper), preferred_element_type=F32)

    def placed_rhs(lev):
        y = s["rhs"][:, R[lev] : R[lev] + V[lev]]
        spread = jnp.concatenate([y] * NP, axis=1)
        col = lax.broadcasted_iota(jnp.int32, (N, W[lev]), 1)
        first = me * V[lev]
        return jnp.where((col >= first) & (col < first + V[lev]), spread, 0.0)

    def nothing():
        pass

    loaded("rhs")
    z = s["rhs"][:, : V[0]]
    col = lax.broadcasted_iota(jnp.int32, (N, V[0]), 1) + (member(0) * W[0] + me * V[0])
    z = jnp.where(col < live(0), z, 0.0)
    s["zs0"][...] = jnp.concatenate([z[8 * r : 8 * r + 8, :] for r in range(N // 8)], axis=1)
    pl.semaphore_wait(barrier, NP - 1 + NL - 1)
    z_copies = []
    for k in range(1, NP):
        device, _ = panel_peer(k)
        z_copies.append(send("zf0", k, s["zs0"], s["zf0"].at[me], device))
    s["zf0"][me] = s["zs0"][...]
    m_copies = {0: send_factor(0)}

    def keep_factor(lev):
        s[f"m{lev}"][...] = factor_rows(lev).astype(BF16)

    keep_factor(3)
    arrive(m_copies[0])
    for q in range(NP):
        part = s["mfull0"][q].astype(BF16)
        for r in range(N // 8):
            start = q * 128 + r * V[0]
            s["w0"][start : start + V[0], :] = part
    arrive(z_copies)
    lane = lax.broadcasted_iota(jnp.int32, (N, 128), 1)
    row = lax.broadcasted_iota(jnp.int32, (N, 128), 0)
    own = lax.div(lane, V[0]) == lax.div(row, 8)
    pieces = []
    for q in range(NP):
        spread = jnp.concatenate([s["zf0"][q]] * (N // 8), axis=0)
        pieces.append(jnp.where(own, spread, 0.0).astype(BF16))
    x = jnp.dot(jnp.concatenate(pieces, axis=1), s["w0"][...], preferred_element_type=F32)

    def ahead0():
        m_copies[1] = send_factor(1)

    def ahead0b():
        keep_factor(4)

    x = leaf_sum(0, x, ahead0, ahead0b)
    out[0, 0] = x
    xb = [x.astype(BF16)]

    for lev in range(1, LEVELS):
        loaded(("tiles", lev))
        total = term(lev, lev - 1, xb[lev - 1])
        if lev > 1:
            total = total + s[f"acc{lev}"][...]

        def ahead_terms(lev=lev):
            for later in range(lev + 1, LEVELS):
                loaded(("tiles", later))
                value = term(later, lev - 1, xb[lev - 1])
                if lev > 1:
                    value = value + s[f"acc{later}"][...]
                s[f"acc{later}"][...] = value

        if lev in GATHER:
            part = placed_rhs(lev) - total
            for r in range(NP):
                s[f"zp{lev}"][r] = part[8 * r : 8 * r + 8, :]
            copies = []
            for k in range(1, NP):
                device, to = panel_peer(k)
                copies.append(
                    send(f"zr{lev}", k, s[f"zp{lev}"].at[to], s[f"zr{lev}"].at[k - 1], device)
                )
            ahead_terms()
            arrive(copies)
            rows = s[f"zp{lev}"][me]
            for k in range(1, NP):
                rows = rows + s[f"zr{lev}"][k - 1]
            col = lax.broadcasted_iota(jnp.int32, (8, W[lev]), 1) + member(lev) * W[lev]
            s[f"zf{lev}"][me] = jnp.where(col < live(lev), rows, 0.0)
            copies = []
            for k in range(1, NP):
                device, _ = panel_peer(k)
                here = s[f"zf{lev}"].at[me]
                copies.append(send(f"zf{lev}", k, here, here, device))
            arrive(m_copies[lev])
            weights = s[f"mfull{lev}"][...].reshape(W[lev], STRIP).astype(BF16)
            arrive(copies)
            zb = s[f"zf{lev}"][...].reshape(N, W[lev]).astype(BF16)
            x = jnp.dot(zb, weights, preferred_element_type=F32)
        else:
            for q in range(NP):
                s[f"zp{lev}"][q] = total[:, q * V[lev] : (q + 1) * V[lev]]
            copies = []
            for k in range(1, NP):
                device, to = panel_peer(k)
                copies.append(
                    send(f"zr{lev}", k, s[f"zp{lev}"].at[to], s[f"zr{lev}"].at[k - 1], device)
                )
            ahead_terms()
            arrive(copies)
            rows = s["rhs"][:, R[lev] : R[lev] + V[lev]] - s[f"zp{lev}"][me]
            for k in range(1, NP):
                rows = rows - s[f"zr{lev}"][k - 1]
            col = lax.broadcasted_iota(jnp.int32, (N, V[lev]), 1)
            col = col + (member(lev) * W[lev] + me * V[lev])
            zb = jnp.where(col < live(lev), rows, 0.0).astype(BF16)
            for q in range(NP):
                weights = s[f"m{lev}"][:, q * STRIP : (q + 1) * STRIP]
                s[f"xp{lev}"][q] = jnp.dot(zb, weights, preferred_element_type=F32)
            copies = []
            for k in range(1, NP):
                device, to = panel_peer(k)
                copies.append(
                    send(f"xq{lev}", k, s[f"xp{lev}"].at[to], s[f"xq{lev}"].at[k - 1], device)
                )
            arrive(copies)
            x = s[f"xp{lev}"][me]
            for k in range(1, NP):
                x = x + s[f"xq{lev}"][k - 1]

        def ahead_factor(lev=lev):
            if lev + 1 in GATHER:
                m_copies[lev + 1] = send_factor(lev + 1)

        x = leaf_sum(lev, x, ahead_factor, nothing)
        out[0, lev] = x
        if lev + 1 < LEVELS:
            xb.append(x.astype(BF16))

    for copy in sent:
        copy.wait_send()


def scratch():
    vmem, dma = pltpu.VMEM, pltpu.SemaphoreType.DMA
    found = [
        ("rhs", vmem((N, R[-1] + V[-1]), F32)),
        ("diag", vmem((R[-1] + V[-1], SEP), BF16)),
        ("tiles", vmem((STRIP, C[-1] + (LEVELS - 1) * W[-1]), BF16)),
        ("load_sem", dma((2 * LEVELS,))),
        ("zs0", vmem((8, 128), F32)),
        ("w0", vmem((NP * 128, STRIP), BF16)),
    ]

    def exchange(tag, count):
        found.append((tag + "_ssem", dma((count,))))
        found.append((tag + "_rsem", dma((count,))))

    for lev in GATHER:
        found.append((f"msend{lev}", vmem((NP, V[lev], STRIP), F32)))
        found.append((f"mfull{lev}", vmem((NP, V[lev], STRIP), F32)))
        exchange(f"m{lev}", NP - 1)
        found.append((f"zf{lev}", vmem((NP, 8, 128 if lev == 0 else W[lev]), F32)))
        exchange(f"zf{lev}", NP - 1)
        if lev:
            found.append((f"zp{lev}", vmem((NP, 8, W[lev]), F32)))
            found.append((f"zr{lev}", vmem((NP - 1, 8, W[lev]), F32)))
            exchange(f"zr{lev}", NP - 1)
    for lev in SPREAD:
        found.append((f"m{lev}", vmem((V[lev], SEP), BF16)))
        found.append((f"zp{lev}", vmem((NP, N, V[lev]), F32)))
        found.append((f"zr{lev}", vmem((NP - 1, N, V[lev]), F32)))
        exchange(f"zr{lev}", NP - 1)
        found.append((f"xp{lev}", vmem((NP, N, STRIP), F32)))
        found.append((f"xq{lev}", vmem((NP - 1, N, STRIP), F32)))
        exchange(f"xq{lev}", NP - 1)
    for lev in range(2, LEVELS):
        found.append((f"acc{lev}", vmem((N, W[lev]), F32)))
    for lev in range(LEVELS):
        g = G[lev]
        if g == 1:
            continue
        if lev in TWO_STEP:
            found.append((f"xs{lev}", vmem((TILES, 8, 128), F32)))
            found.append((f"xr{lev}", vmem((g - 1, TILES // g, 8, 128), F32)))
            found.append((f"xf{lev}", vmem((TILES, 8, 128), F32)))
            exchange(f"xf{lev}", g - 1)
        else:
            found.append((f"xs{lev}", vmem((N, STRIP), F32)))
            found.append((f"xr{lev}", vmem((g - 1, N, STRIP), F32)))
        exchange(f"xs{lev}", g - 1)
    return found


def per_device(adjoint_rhs, panel_tiles, diag_inverse, front_sizes):
    anywhere = pl.BlockSpec(memory_space=pl.ANY)
    return pl.pallas_call(
        kernel,
        name="solve",
        out_shape=jax.ShapeDtypeStruct((1, LEVELS, N, STRIP), F32),
        in_specs=[pl.BlockSpec(memory_space=pltpu.SMEM), anywhere, anywhere, anywhere],
        out_specs=pl.BlockSpec(memory_space=pltpu.VMEM),
        scratch_shapes=[spec for _, spec in scratch()],
        compiler_params=pltpu.CompilerParams(
            collective_id=0, has_side_effects=True, vmem_limit_bytes=56 << 20
        ),
    )(front_sizes, adjoint_rhs, panel_tiles, diag_inverse)


def solution(mesh):
    in_specs = (P("leaf", None, "panel"), P("leaf", "panel", None), P("leaf", "panel", None), P())
    out_specs = P("leaf", None, None, "panel")
    return jax.shard_map(
        per_device, mesh=mesh, in_specs=in_specs, out_specs=out_specs, check_vma=False
    )
```
